512 devices in a mesh: grp: 128 (over x, z, core), lev: 4 (over y).
Axes of the slice: x: 4, y: 4, z: 16, core: 2. Of those that a mesh axis runs over, the one named last changes fastest.
Arguments:
- spectrum: float32 [16, 640, 2, 640], P('lev', 'grp'), may hold values from -6 to 6
- wave_slot: int32 [640], replicated, may hold values from 0 to 639, each once
Outputs:
- new_spectrum: float32 [16, 640, 2, 640], P('lev', 'grp')
- products: float32 [16, 1024, 1440], P('lev', 'grp')
The draws below stay inside these ranges and needn't reach their ends.
Inputs may be any that keep to these rules, and one draw needn't show every extreme that they name: Row s of the spectral arrays holds zonal wavenumber wave_slot[s]; every wavenumber below 640 appears exactly once.
All inputs are finite; a program needn't handle non-finite values.
Results may differ from the reference program's by a relative error of at most 0.0003.
Values sent between devices are 32-bit elements; how exact they have to be, the bound alone decides.
A program may use at most 128 MiB of HBM per device.

```python
import math
import jax
import jax.numpy as jnp
from jax import lax

MM = 640
NN = 640
NLON = 1440
LEVELS = 16
NLAT = 1024


def level_of(rng, dims, split, smallest, largest):
    loudness, own = 1.0, jax.random.fold_in(rng, 6)
    for position, parts in split:
        draws = jnp.exp(jax.random.uniform(jax.random.fold_in(own, position), (parts,), jnp.float32, smallest / len(split), largest / len(split)))
        loudness = loudness * jnp.repeat(draws, dims[position] // parts).reshape([-1 if axis == position else 1 for axis in range(len(dims))])
    return loudness


def scatter_about(rng, shape, width, reach, shards=(), kind=jnp.bfloat16):
    values = width * jax.random.normal(rng, shape, jnp.float32)
    if shards:
        values = values * level_of(rng, shape, shards, -0.22, 0.18)
    return jnp.clip(values, -reach, reach).astype(kind)


def setup_inputs(seed: int = 0) -> dict:
    arg_keys = jax.random.split(jax.random.key(seed), 3)
    return {
        "spectrum": scatter_about(arg_keys[0], (LEVELS, MM, 2, NN), 1.0, 6.0, ((0, 4), (1, 128)), jnp.float32),
        "wave_slot": jax.random.permutation(arg_keys[1], MM).astype(jnp.int32),
    }


def lat_basis(wavenumbers, lat_count, degrees):
    rows = jnp.arange(lat_count, dtype=jnp.int32)
    orders = jnp.arange(degrees, dtype=jnp.int32)
    is_odd = wavenumbers % 2
    multiple = orders[None, :] + is_odd[:, None]
    phase_steps = (multiple[:, None, :] * (2 * rows[None, :, None] + 1) - is_odd[:, None, None] * lat_count) % (4 * lat_count)
    values = jnp.cos(phase_steps.astype(jnp.float32) * (math.pi / (2 * lat_count)))
    return jnp.where(orders[None, None, :] >= wavenumbers[:, None, None], values, jnp.zeros_like(values))


def lon_tables(wavenumbers, lon_count):
    cols = jnp.arange(lon_count, dtype=jnp.int32)
    phase_steps = (wavenumbers[:, None] * cols[None, :]) % lon_count
    angles = phase_steps.astype(jnp.float32) * (2.0 * math.pi / lon_count)
    return jnp.stack([jnp.cos(angles), -jnp.sin(angles)])


def wave_weight(wavenumbers):
    return jnp.where(wavenumbers == 0, 1.0, 2.0).astype(jnp.float32)


def longitude_synth(fourier, wavenumbers, tables):
    weighted = fourier * wave_weight(wavenumbers)[None, None, :, None]
    return jnp.einsum("lcsj,csi->lji", weighted, tables, precision=lax.Precision.HIGHEST)


def longitude_analysis(paired, tables):
    return jnp.einsum("lji,csi->lcsj", paired, tables, precision=lax.Precision.HIGHEST) / NLON


def meridional_synth(spectrum, wavenumbers):
    def per_slot(args):
        coefficients, wavenumber = args
        basis_rows = lat_basis(wavenumber[None], NLAT, NN)[0]
        return jnp.einsum("lcn,jn->lcj", coefficients, basis_rows, precision=lax.Precision.HIGHEST) / NN
    result = lax.map(per_slot, (jnp.moveaxis(spectrum, 1, 0), wavenumbers))
    return jnp.transpose(result, (1, 2, 0, 3))


def meridional_analysis(fourier_back, wavenumbers):
    def per_slot(args):
        coefficients, wavenumber = args
        basis_rows = lat_basis(wavenumber[None], NLAT, NN)[0]
        return jnp.einsum("lcj,jn->lcn", coefficients, basis_rows, precision=lax.Precision.HIGHEST) * (2.0 * NN / NLAT)
    result = lax.map(per_slot, (jnp.moveaxis(fourier_back, 2, 0), wavenumbers))
    return jnp.transpose(result, (1, 0, 2, 3))


def reference(spectrum, wave_slot):
    tables = lon_tables(wave_slot, NLON)
    fourier = meridional_synth(spectrum, wave_slot)
    grid_values = longitude_synth(fourier, wave_slot, tables)
    partner = jnp.roll(grid_values, LEVELS // 2, axis=0)
    paired = grid_values * partner + grid_values
    fourier_back = longitude_analysis(paired, tables)
    new_spectrum = meridional_analysis(fourier_back, wave_slot)
    fourier_new = meridional_synth(new_spectrum, wave_slot)
    products = longitude_synth(fourier_new, wave_slot, tables)
    return new_spectrum, products
```

```python
import functools
import math

import jax
import jax.numpy as jnp
import numpy as np
from jax import lax
from jax.experimental import pallas as pl
from jax.experimental.pallas import tpu as pltpu
from jax.sharding import PartitionSpec as P

NLON = 1440
LANES = 1536
NN = 640
NLAT = 1024
CHIPS = 64
SLOTS = 10
MESH = pl.DeviceIdType.MESH
F32 = jnp.float32
BF16 = jnp.bfloat16


def meridional_parts():
    chips = np.arange(CHIPS)
    coarse, fine = [], []
    odd_rows = 16 * np.arange(2)[:, None] + 2 * np.arange(8)[None, :] + 1
    for shift in range(2):
        k = np.arange(NN) + shift
        a = 2.0 * np.pi * ((chips[:, None] * k[None, :]) % 128) / 128.0
        b = np.pi * ((odd_rows[:, :, None] * k) % 4096) / 2048.0
        coarse += [np.cos(a), np.sin(a)]
        fine += [np.cos(b), np.sin(b)]
    return np.stack(coarse).astype(np.float32), np.stack(fine, axis=2).astype(np.float32)


def split(value):
    high = value.astype(BF16)
    return high, (value - high.astype(F32)).astype(BF16)


def dot_nn(a, b):
    return lax.dot_general(a, b, (((1,), (0,)), ((), ())), preferred_element_type=F32)


def dot_nt(a, b):
    return lax.dot_general(a, b, (((1,), (1,)), ((), ())), preferred_element_type=F32)


def cos_sin(steps):
    turn = steps - 1440.0 * jnp.floor((steps + 0.5) * (1.0 / 1440.0))
    quarter = jnp.floor((turn + 180.0) * (1.0 / 360.0) + 1e-4)
    t = (turn - 360.0 * quarter) * (2.0 * math.pi / 1440.0)
    u = t * t
    s = t * (1.0 + u * (-1.0 / 6 + u * (1.0 / 120 + u * (-1.0 / 5040 + u * (1.0 / 362880)))))
    c = 1.0 + u * (-0.5 + u * (1.0 / 24 + u * (-1.0 / 720 + u * (1.0 / 40320 + u * (-1.0 / 3628800)))))
    swap = (quarter == 1.0) | (quarter == 3.0)
    cos, sin = jnp.where(swap, s, c), jnp.where(swap, c, s)
    cos = jnp.where((quarter == 1.0) | (quarter == 2.0), -cos, cos)
    sin = jnp.where((quarter == 2.0) | (quarter == 3.0), -sin, sin)
    return cos, sin


def kernel(
    x_ref, waves_ref, wave_scalars, coarse_ref, fine_ref,
    new_ref, products_ref,
    spec, part, part_in, mer_hi, mer_lo, weights_x, lon_hi, lon_lo, weights_p,
    send1, recv1, send2, recv2, send3, recv3, grid, grid_in, final,
    pair_send, pair_recv, all_send, all_recv, lev_send, lev_recv,
):
    me, level = lax.axis_index("grp"), lax.axis_index("lev")
    core, chip = lax.rem(me, 2), me // 2
    sibling = {"grp": 2 * chip + 1 - core}
    partner = {"lev": lax.rem(level + 2, 4)}

    def peer(step):
        return lax.rem(chip + step, CHIPS)

    barrier = pltpu.get_barrier_semaphore()

    @pl.loop(1, CHIPS)
    def _(step):
        pl.semaphore_signal(barrier, inc=1, device_id={"grp": 2 * peer(step) + core}, device_id_type=MESH)

    pl.semaphore_signal(barrier, inc=1, device_id=sibling, device_id_type=MESH)
    pl.semaphore_signal(barrier, inc=1, device_id=partner, device_id_type=MESH)

    for s in range(5):
        for c in range(2):
            spec[5 * core + s, 4 * c:4 * c + 4, :] = x_ref[:, s, c, :]

    @pl.loop(0, 8)
    def _(row):
        fine = fine_ref[core, row]
        for parity in range(2):
            fc, fs = fine[2 * parity:2 * parity + 1], fine[2 * parity + 1:2 * parity + 2]
            for block in range(4):
                rows = slice(16 * block, 16 * block + 16)
                cc, cs = coarse_ref[2 * parity, rows, :], coarse_ref[2 * parity + 1, rows, :]
                value = cc * fc - cs * fs if parity == 0 else cs * fc + cc * fs
                high, low = split(value)
                where = pl.ds(pl.multiple_of(row * CHIPS + 16 * block, 16), 16)
                columns = slice(NN * parity, NN * parity + NN)
                mer_hi[where, columns] = high
                mer_lo[where, columns] = low

    lane = lax.broadcasted_iota(jnp.int32, (16, 128), 1)
    lane_f = lane.astype(F32)
    for s in range(SLOTS):
        @pl.loop(0, 4)
        def _(block):
            wave = waves_ref[pl.ds(pl.multiple_of(16 * block, 16), 16), s:s + 1] + jnp.zeros((16, 128), F32)
            cos, sin = cos_sin(wave * lane_f)
            turn_cos, turn_sin = cos_sin(wave * 128.0)
            first = pl.multiple_of(s * CHIPS + 16 * block, 16)
            second = pl.multiple_of((SLOTS + s) * CHIPS + 16 * block, 16)
            for a in range(LANES // 128):
                columns = slice(128 * a, 128 * a + 128)
                put_cos, put_sin = cos, -sin
                if 128 * a + 128 > NLON:
                    inside = lane < NLON - 128 * a
                    put_cos, put_sin = jnp.where(inside, put_cos, 0.0), jnp.where(inside, put_sin, 0.0)
                lon_hi[pl.ds(first, 16), columns], lon_lo[pl.ds(first, 16), columns] = split(put_cos)
                lon_hi[pl.ds(second, 16), columns], lon_lo[pl.ds(second, 16), columns] = split(put_sin)
                if 128 * a + 128 < LANES:
                    cos, sin = cos * turn_cos - sin * turn_sin, sin * turn_cos + cos * turn_sin

    weights_x[...] = jnp.zeros_like(weights_x)
    weights_p[...] = jnp.zeros_like(weights_p)

    pl.semaphore_wait(barrier, CHIPS + 1)

    def pair_copy(index, source, target):
        return pltpu.make_async_remote_copy(
            src_ref=source, dst_ref=target, send_sem=pair_send.at[index], recv_sem=pair_recv.at[index],
            device_id=sibling, device_id_type=MESH)

    mine = spec.at[pl.ds(5 * core, 5)]
    copy = pair_copy(0, mine, mine)
    copy.start()
    copy.wait()

    degree = lax.broadcasted_iota(jnp.int32, (8, NN), 1)
    lane64 = lax.broadcasted_iota(jnp.int32, (CHIPS, 128), 1)
    lane8 = lax.broadcasted_iota(jnp.int32, (8, 128), 1)
    sub8 = lax.broadcasted_iota(jnp.int32, (8, 128), 0)

    def slot_wave(s):
        return wave_scalars[SLOTS * chip + s]

    def exchange(index, out, inbox):
        @pl.loop(1, CHIPS)
        def _(step):
            to = peer(step)
            pltpu.make_async_remote_copy(
                src_ref=out.at[to], dst_ref=inbox.at[chip], send_sem=all_send.at[index], recv_sem=all_recv.at[index],
                device_id={"grp": 2 * to + core}, device_id_type=MESH).start()

        inbox[chip] = out[chip]
        arrived = inbox.at[pl.ds(0, CHIPS - 1)]
        pltpu.make_async_copy(arrived, arrived, all_recv.at[index]).wait()
        left = out.at[pl.ds(0, CHIPS - 1)]
        pltpu.make_async_copy(left, left, all_send.at[index]).wait()

    def meridional_synth(source, out):
        for parity in range(2):
            for half in range(5):
                rows = []
                for s in (2 * half, 2 * half + 1):
                    wave = slot_wave(s)
                    odd = wave % 2
                    chosen = odd if parity else 1 - odd
                    scale = chosen.astype(F32) * jnp.where(wave == 0, 1.0 / NN, 2.0 / NN)
                    rows.append(jnp.where(degree >= wave, source[s] * scale, 0.0))
                high, low = split(jnp.concatenate(rows, axis=0))
                columns = slice(NN * parity, NN * parity + NN)
                weights_x[16 * half:16 * half + 16, columns] = high
                weights_x[128 + 16 * half:128 + 16 * half + 16, columns] = low
        both = dot_nt(mer_hi[...], weights_x[...])
        value = both[:, :128] + both[:, 128:] + dot_nt(mer_lo[...], weights_x[:128, :])
        tiles = [None] * 5

        def put(t, piece):
            tiles[t] = piece if tiles[t] is None else tiles[t] + piece

        for row in range(8):
            t, offset = divmod(80 * row, 128)
            piece = value[CHIPS * row:CHIPS * row + CHIPS, :]
            if offset:
                piece = pltpu.roll(piece, offset, 1)
            if offset + 80 > 128:
                put(t, jnp.where(lane64 >= offset, piece, 0.0))
                put(t + 1, jnp.where(lane64 < offset, piece, 0.0))
            else:
                put(t, piece)
        for t in range(5):
            out[:, t, :] = tiles[t]

    def turned(inbox):
        result = []
        for t in range(5):
            block = inbox[:, t, :]
            result.append(jnp.concatenate([block, block], axis=0).T)
        return result

    def longitude_operand(inbox):
        tiles = turned(inbox)

        def group(row, s):
            t, offset = divmod(80 * row + 8 * s, 128)
            return tiles[t][offset:offset + 8, :]

        real, imag = [], []
        for pair in range(4):
            real_row, imag_row = [], []
            for half in range(5):
                a, b = (
                    jnp.where(lane8 < 64, group(row, 2 * half), group(row, 2 * half + 1))
                    for row in (2 * pair, 2 * pair + 1))
                real_row.append(jnp.where(sub8 < 4, a, pltpu.roll(b, 4, 0)))
                imag_row.append(jnp.where(sub8 < 4, pltpu.roll(a, 4, 0), b))
            real.append(jnp.concatenate(real_row, axis=1))
            imag.append(jnp.concatenate(imag_row, axis=1))
        value = jnp.concatenate([jnp.concatenate(real, axis=0), jnp.concatenate(imag, axis=0)], axis=1)
        return split(value)

    def longitude_synth(high, low, columns):
        both = dot_nn(jnp.concatenate([high, low], axis=0), lon_hi[:, columns])
        return both[:32] + both[32:] + dot_nn(high, lon_lo[:, columns])

    meridional_synth(spec, send1)
    exchange(0, send1, recv1)
    high, low = longitude_operand(recv1)
    copies = []
    for a in range(3):
        grid[a] = longitude_synth(high, low, slice(512 * a, 512 * a + 512))
        copy = pltpu.make_async_remote_copy(
            src_ref=grid.at[a], dst_ref=grid_in.at[a], send_sem=lev_send.at[a], recv_sem=lev_recv.at[a],
            device_id=partner, device_id_type=MESH)
        copy.start()
        copies.append(copy)
    for a in range(3):
        copies[a].wait()
        here = grid[a]
        high, low = split(here * grid_in[a] + here)
        weights_p[0:32, 512 * a:512 * a + 512] = high
        weights_p[128:160, 512 * a:512 * a + 512] = low

    both = dot_nt(lon_hi[...], weights_p[...])
    value = both[:, :128] + both[:, 128:] + dot_nt(lon_lo[...], weights_p[:128, :])
    for t in range(5):
        tile = None
        for s in range(2):
            for c in range(2):
                first = (c * SLOTS + 2 * t + s) * CHIPS
                piece = value[first:first + CHIPS, :]
                offset = 64 * s + 32 * c
                piece = pltpu.roll(piece, offset, 1) if offset else piece
                tile = piece if tile is None else tile + piece
        send2[:, t, :] = tile
    exchange(1, send2, recv2)

    tiles = turned(recv2)
    rows = []
    for s in range(SLOTS):
        row = []
        for pair in range(4):
            a, b = (
                tiles[s // 2][64 * (s % 2) + 32 * c + 8 * pair:64 * (s % 2) + 32 * c + 8 * pair + 8, :] for c in range(2))
            left = jnp.where(sub8 < 4, a, pltpu.roll(b, 4, 0))
            right = jnp.where(sub8 < 4, pltpu.roll(a, 4, 0), b)
            row.append(jnp.where(lane8 < 64, left, right))
        rows.append(jnp.concatenate(row, axis=1))
    high, low = split(jnp.concatenate(rows, axis=0))
    both = dot_nn(jnp.concatenate([high, low], axis=0), mer_hi[...])
    value = both[:80] + both[80:] + dot_nn(high, mer_lo[...])
    for s in range(SLOTS):
        wave = slot_wave(s)
        odd = (wave % 2).astype(F32)
        chosen = value[8 * s:8 * s + 8, :NN] * (1.0 - odd) + value[8 * s:8 * s + 8, NN:] * odd
        part[s] = jnp.where(degree >= wave, chosen * (2.0 * NN / NLAT / NLON), 0.0)
    copy = pair_copy(1, part, part_in)
    copy.start()
    copy.wait()
    for s in range(SLOTS):
        spec[s] = part[s] + part_in[s]
    for s in range(5):
        for c in range(2):
            new_ref[:, s, c, :] = spec[5 * core + s, 4 * c:4 * c + 4, :]

    meridional_synth(spec, send3)
    exchange(2, send3, recv3)
    high, low = longitude_operand(recv3)
    for a in range(3):
        value = longitude_synth(high, low, slice(512 * a, 512 * a + 512))
        for b in range(4):
            tile = 4 * a + b
            width = min(128, NLON - 128 * tile)
            final[tile] = value[:, 128 * b:128 * b + 128]
            for l in range(4):
                products_ref[l, :, 128 * tile:128 * tile + width] = final[tile, pl.ds(l, 8, stride=4), :][:, :width]


def on_device(spectrum, wave_slot):
    coarse, fine = meridional_parts()
    vmem, smem = pl.BlockSpec(memory_space=pltpu.VMEM), pl.BlockSpec(memory_space=pltpu.SMEM)
    message = pltpu.VMEM((CHIPS, 5, 128), F32)
    return pl.pallas_call(
        kernel,
        out_shape=(
            jax.ShapeDtypeStruct((4, 5, 2, NN), F32),
            jax.ShapeDtypeStruct((4, 8, NLON), F32),
        ),
        in_specs=[vmem, vmem, smem, vmem, vmem],
        out_specs=(vmem, vmem),
        scratch_shapes=[
            pltpu.VMEM((SLOTS, 8, NN), F32),
            pltpu.VMEM((SLOTS, 8, NN), F32),
            pltpu.VMEM((SLOTS, 8, NN), F32),
            pltpu.VMEM((8 * CHIPS, 2 * NN), BF16),
            pltpu.VMEM((8 * CHIPS, 2 * NN), BF16),
            pltpu.VMEM((256, 2 * NN), BF16),
            pltpu.VMEM((2 * SLOTS * CHIPS, LANES), BF16),
            pltpu.VMEM((2 * SLOTS * CHIPS, LANES), BF16),
            pltpu.VMEM((256, LANES), BF16),
            message, message, message, message, message, message,
            pltpu.VMEM((3, 32, 512), F32),
            pltpu.VMEM((3, 32, 512), F32),
            pltpu.VMEM((12, 32, 128), F32),
            pltpu.SemaphoreType.DMA((2,)),
            pltpu.SemaphoreType.DMA((2,)),
            pltpu.SemaphoreType.DMA((3,)),
            pltpu.SemaphoreType.DMA((3,)),
            pltpu.SemaphoreType.DMA((3,)),
            pltpu.SemaphoreType.DMA((3,)),
        ],
        compiler_params=pltpu.CompilerParams(collective_id=0, has_side_effects=True, vmem_limit_bytes=48 << 20),
    )(spectrum, wave_slot.reshape(CHIPS, SLOTS).astype(F32), wave_slot, jnp.asarray(coarse), jnp.asarray(fine))


def solution(mesh):
    return jax.shard_map(
        on_device,
        mesh=mesh,
        in_specs=(P("lev", "grp", None, None), P()),
        out_specs=(P("lev", "grp", None, None), P("lev", "grp", None)),
        check_vma=False,
    )
```

```python
import functools
import math

import jax
import jax.numpy as jnp
import numpy as np
from jax import lax
from jax.experimental import pallas as pl
from jax.experimental.pallas import tpu as pltpu
from jax.sharding import PartitionSpec as P

NLON = 1440
LANES = 1536
NN = 640
NLAT = 1024
CHIPS = 64
SLOTS = 10
MESH = pl.DeviceIdType.MESH
F32 = jnp.float32
BF16 = jnp.bfloat16


def meridional_parts():
    chips = np.arange(CHIPS)
    coarse, fine = [], []
    odd_rows = 16 * np.arange(2)[:, None] + 2 * np.arange(8)[None, :] + 1
    for shift in range(2):
        k = np.arange(NN) + shift
        a = 2.0 * np.pi * ((chips[:, None] * k[None, :]) % 128) / 128.0
        b = np.pi * ((odd_rows[:, :, None] * k) % 4096) / 2048.0
        coarse += [np.cos(a), np.sin(a)]
        fine += [np.cos(b), np.sin(b)]
    return np.stack(coarse).astype(np.float32), np.stack(fine, axis=2).astype(np.float32)


def split(value):
    high = value.astype(BF16)
    return high, (value - high.astype(F32)).astype(BF16)


def dot_nn(a, b):
    return lax.dot_general(a, b, (((1,), (0,)), ((), ())), preferred_element_type=F32)


def dot_nt(a, b):
    return lax.dot_general(a, b, (((1,), (1,)), ((), ())), preferred_element_type=F32)


def cos_sin(steps):
    turn = steps - 1440.0 * jnp.floor((steps + 0.5) * (1.0 / 1440.0))
    quarter = jnp.floor((turn + 180.0) * (1.0 / 360.0) + 1e-4)
    t = (turn - 360.0 * quarter) * (2.0 * math.pi / 1440.0)
    u = t * t
    s = t * (1.0 + u * (-1.0 / 6 + u * (1.0 / 120 + u * (-1.0 / 5040 + u * (1.0 / 362880)))))
    c = 1.0 + u * (-0.5 + u * (1.0 / 24 + u * (-1.0 / 720 + u * (1.0 / 40320 + u * (-1.0 / 3628800)))))
    swap = (quarter == 1.0) | (quarter == 3.0)
    cos, sin = jnp.where(swap, s, c), jnp.where(swap, c, s)
    cos = jnp.where((quarter == 1.0) | (quarter == 2.0), -cos, cos)
    sin = jnp.where((quarter == 2.0) | (quarter == 3.0), -sin, sin)
    return cos, sin


def kernel(
    x_in, waves_in, scalars_in, coarse_in, fine_in,
    new_ref, products_ref,
    x_ref, waves_ref, wave_scalars, coarse_ref, fine_ref, load_sem,
    spec, part, part_in, mer_hi, mer_lo, weights_x, lon_hi, lon_lo, weights_p,
    send1, recv1, send2, recv2, send3, recv3, grid, grid_in, final,
    pair_send, pair_recv, all_send, all_recv, lev_send, lev_recv,
):
    me, level = lax.axis_index("grp"), lax.axis_index("lev")
    core, chip = lax.rem(me, 2), me // 2
    sibling = {"grp": 2 * chip + 1 - core}
    partner = {"lev": lax.rem(level + 2, 4)}

    def peer(step):
        turn = (step - 1) // 4
        along_z = jnp.where(turn % 2 == 0, 8 + turn // 2, 8 - (turn + 1) // 2)
        along_x = 3 - (step - 1) % 4
        return lax.rem(chip // 16 + along_x, 4) * 16 + lax.rem(chip % 16 + along_z, 16)

    loads = [
        pltpu.make_async_copy(source, target, load_sem.at[index])
        for index, (source, target) in enumerate((
            (x_in, x_ref), (scalars_in, wave_scalars), (coarse_in, coarse_ref), (fine_in.at[core], fine_ref),
            (waves_in, waves_ref)))]
    for load in loads:
        load.start()
    barrier = pltpu.get_barrier_semaphore()

    @pl.loop(1, CHIPS)
    def _(step):
        pl.semaphore_signal(barrier, inc=1, device_id={"grp": 2 * peer(step) + core}, device_id_type=MESH)

    pl.semaphore_signal(barrier, inc=1, device_id=sibling, device_id_type=MESH)
    pl.semaphore_signal(barrier, inc=1, device_id=partner, device_id_type=MESH)

    loads[0].wait()
    loads[1].wait()
    for s in range(5):
        for c in range(2):
            spec[5 * core + s, 4 * c:4 * c + 4, :] = x_ref[:, s, c, :]

    loads[2].wait()
    loads[3].wait()
    @pl.loop(0, 8)
    def _(row):
        fine = fine_ref[row]
        for parity in range(2):
            fc, fs = fine[2 * parity:2 * parity + 1], fine[2 * parity + 1:2 * parity + 2]
            for block in range(4):
                rows = slice(16 * block, 16 * block + 16)
                cc, cs = coarse_ref[2 * parity, rows, :], coarse_ref[2 * parity + 1, rows, :]
                value = cc * fc - cs * fs if parity == 0 else cs * fc + cc * fs
                high, low = split(value)
                where = pl.ds(pl.multiple_of(row * CHIPS + 16 * block, 16), 16)
                columns = slice(NN * parity, NN * parity + NN)
                mer_hi[where, columns] = high
                mer_lo[where, columns] = low

    loads[4].wait()
    lane = lax.broadcasted_iota(jnp.int32, (16, 128), 1)
    lane_f = lane.astype(F32)
    for s in range(SLOTS):
        @pl.loop(0, 4)
        def _(block):
            wave = waves_ref[pl.ds(pl.multiple_of(16 * block, 16), 16), s:s + 1].astype(F32) + jnp.zeros((16, 128), F32)
            cos, sin = cos_sin(wave * lane_f)
            turn_cos, turn_sin = cos_sin(wave * 128.0)
            first = pl.multiple_of(s * CHIPS + 16 * block, 16)
            second = pl.multiple_of((SLOTS + s) * CHIPS + 16 * block, 16)
            for a in range(LANES // 128):
                columns = slice(128 * a, 128 * a + 128)
                put_cos, put_sin = cos, -sin
                if 128 * a + 128 > NLON:
                    inside = lane < NLON - 128 * a
                    put_cos, put_sin = jnp.where(inside, put_cos, 0.0), jnp.where(inside, put_sin, 0.0)
                lon_hi[pl.ds(first, 16), columns], lon_lo[pl.ds(first, 16), columns] = split(put_cos)
                lon_hi[pl.ds(second, 16), columns], lon_lo[pl.ds(second, 16), columns] = split(put_sin)
                if 128 * a + 128 < LANES:
                    cos, sin = cos * turn_cos - sin * turn_sin, sin * turn_cos + cos * turn_sin

    weights_x[...] = jnp.zeros_like(weights_x)
    weights_p[...] = jnp.zeros_like(weights_p)

    pl.semaphore_wait(barrier, CHIPS + 1)

    def pair_copy(index, source, target):
        return pltpu.make_async_remote_copy(
            src_ref=source, dst_ref=target, send_sem=pair_send.at[index], recv_sem=pair_recv.at[index],
            device_id=sibling, device_id_type=MESH)

    mine = spec.at[pl.ds(5 * core, 5)]
    copy = pair_copy(0, mine, mine)
    copy.start()
    copy.wait()

    degree = lax.broadcasted_iota(jnp.int32, (8, NN), 1)
    lane64 = lax.broadcasted_iota(jnp.int32, (CHIPS, 128), 1)
    lane8 = lax.broadcasted_iota(jnp.int32, (8, 128), 1)
    sub8 = lax.broadcasted_iota(jnp.int32, (8, 128), 0)

    def slot_wave(s):
        return wave_scalars[SLOTS * chip + s]

    def exchange(index, out, inbox):
        @pl.loop(1, CHIPS)
        def _(step):
            to = peer(step)
            pltpu.make_async_remote_copy(
                src_ref=out.at[to], dst_ref=inbox.at[chip], send_sem=all_send.at[index], recv_sem=all_recv.at[index],
                device_id={"grp": 2 * to + core}, device_id_type=MESH).start()

        inbox[chip] = out[chip]
        arrived = inbox.at[pl.ds(0, CHIPS - 1)]
        pltpu.make_async_copy(arrived, arrived, all_recv.at[index]).wait()
        left = out.at[pl.ds(0, CHIPS - 1)]
        pltpu.make_async_copy(left, left, all_send.at[index]).wait()

    def meridional_synth(source, out):
        for parity in range(2):
            for half in range(5):
                rows = []
                for s in (2 * half, 2 * half + 1):
                    wave = slot_wave(s)
                    odd = wave % 2
                    chosen = odd if parity else 1 - odd
                    scale = chosen.astype(F32) * jnp.where(wave == 0, 1.0 / NN, 2.0 / NN)
                    rows.append(jnp.where(degree >= wave, source[s] * scale, 0.0))
                high, low = split(jnp.concatenate(rows, axis=0))
                columns = slice(NN * parity, NN * parity + NN)
                weights_x[16 * half:16 * half + 16, columns] = high
                weights_x[128 + 16 * half:128 + 16 * half + 16, columns] = low
        both = dot_nt(mer_hi[...], weights_x[...])
        value = both[:, :128] + both[:, 128:] + dot_nt(mer_lo[...], weights_x[:128, :])
        tiles = [None] * 5

        def put(t, piece):
            tiles[t] = piece if tiles[t] is None else tiles[t] + piece

        for row in range(8):
            t, offset = divmod(80 * row, 128)
            piece = value[CHIPS * row:CHIPS * row + CHIPS, :]
            if offset:
                piece = pltpu.roll(piece, offset, 1)
            if offset + 80 > 128:
                put(t, jnp.where(lane64 >= offset, piece, 0.0))
                put(t + 1, jnp.where(lane64 < offset, piece, 0.0))
            else:
                put(t, piece)
        for t in range(5):
            out[:, t, :] = tiles[t]

    def turned(inbox):
        result = []
        for t in range(5):
            block = inbox[:, t, :]
            result.append(jnp.concatenate([block, block], axis=0).T)
        return result

    def longitude_operand(inbox):
        tiles = turned(inbox)

        def group(row, s):
            t, offset = divmod(80 * row + 8 * s, 128)
            return tiles[t][offset:offset + 8, :]

        real, imag = [], []
        for pair in range(4):
            real_row, imag_row = [], []
            for half in range(5):
                a, b = (
                    jnp.where(lane8 < 64, group(row, 2 * half), group(row, 2 * half + 1))
                    for row in (2 * pair, 2 * pair + 1))
                real_row.append(jnp.where(sub8 < 4, a, pltpu.roll(b, 4, 0)))
                imag_row.append(jnp.where(sub8 < 4, pltpu.roll(a, 4, 0), b))
            real.append(jnp.concatenate(real_row, axis=1))
            imag.append(jnp.concatenate(imag_row, axis=1))
        value = jnp.concatenate([jnp.concatenate(real, axis=0), jnp.concatenate(imag, axis=0)], axis=1)
        return split(value)

    def longitude_synth(high, low, columns):
        both = dot_nn(jnp.concatenate([high, low], axis=0), lon_hi[:, columns])
        return both[:32] + both[32:] + dot_nn(high, lon_lo[:, columns])

    meridional_synth(spec, send1)
    exchange(0, send1, recv1)
    high, low = longitude_operand(recv1)
    copies = []
    for a in range(3):
        grid[a] = longitude_synth(high, low, slice(512 * a, 512 * a + 512))
        copy = pltpu.make_async_remote_copy(
            src_ref=grid.at[a], dst_ref=grid_in.at[a], send_sem=lev_send.at[a], recv_sem=lev_recv.at[a],
            device_id=partner, device_id_type=MESH)
        copy.start()
        copies.append(copy)
    for a in range(3):
        copies[a].wait()
        here = grid[a]
        high, low = split(here * grid_in[a] + here)
        weights_p[0:32, 512 * a:512 * a + 512] = high
        weights_p[128:160, 512 * a:512 * a + 512] = low

    both = dot_nt(lon_hi[...], weights_p[...])
    value = both[:, :128] + both[:, 128:] + dot_nt(lon_lo[...], weights_p[:128, :])
    for t in range(5):
        tile = None
        for s in range(2):
            for c in range(2):
                first = (c * SLOTS + 2 * t + s) * CHIPS
                piece = value[first:first + CHIPS, :]
                offset = 64 * s + 32 * c
                piece = pltpu.roll(piece, offset, 1) if offset else piece
                tile = piece if tile is None else tile + piece
        send2[:, t, :] = tile
    exchange(1, send2, recv2)

    tiles = turned(recv2)
    rows = []
    for s in range(SLOTS):
        row = []
        for pair in range(4):
            a, b = (
                tiles[s // 2][64 * (s % 2) + 32 * c + 8 * pair:64 * (s % 2) + 32 * c + 8 * pair + 8, :] for c in range(2))
            left = jnp.where(sub8 < 4, a, pltpu.roll(b, 4, 0))
            right = jnp.where(sub8 < 4, pltpu.roll(a, 4, 0), b)
            row.append(jnp.where(lane8 < 64, left, right))
        rows.append(jnp.concatenate(row, axis=1))
    high, low = split(jnp.concatenate(rows, axis=0))
    both = dot_nn(jnp.concatenate([high, low], axis=0), mer_hi[...])
    value = both[:80] + both[80:] + dot_nn(high, mer_lo[...])
    for s in range(SLOTS):
        wave = slot_wave(s)
        odd = (wave % 2).astype(F32)
        chosen = value[8 * s:8 * s + 8, :NN] * (1.0 - odd) + value[8 * s:8 * s + 8, NN:] * odd
        part[s] = jnp.where(degree >= wave, chosen * (2.0 * NN / NLAT / NLON), 0.0)
    copy = pair_copy(1, part, part_in)
    copy.start()
    copy.wait()
    for s in range(SLOTS):
        spec[s] = part[s] + part_in[s]
    for s in range(5):
        for c in range(2):
            new_ref[:, s, c, :] = spec[5 * core + s, 4 * c:4 * c + 4, :]

    meridional_synth(spec, send3)
    exchange(2, send3, recv3)
    high, low = longitude_operand(recv3)
    for a in range(3):
        value = longitude_synth(high, low, slice(512 * a, 512 * a + 512))
        for b in range(4):
            tile = 4 * a + b
            width = min(128, NLON - 128 * tile)
            final[tile] = value[:, 128 * b:128 * b + 128]
            for l in range(4):
                products_ref[l, :, 128 * tile:128 * tile + width] = final[tile, pl.ds(l, 8, stride=4), :][:, :width]


def on_device(spectrum, wave_slot):
    coarse, fine = meridional_parts()
    vmem, anywhere = pl.BlockSpec(memory_space=pltpu.VMEM), pl.BlockSpec(memory_space=pl.ANY)
    message = pltpu.VMEM((CHIPS, 5, 128), F32)
    return pl.pallas_call(
        kernel,
        out_shape=(
            jax.ShapeDtypeStruct((4, 5, 2, NN), F32),
            jax.ShapeDtypeStruct((4, 8, NLON), F32),
        ),
        in_specs=[anywhere] * 5,
        out_specs=(vmem, vmem),
        scratch_shapes=[
            pltpu.VMEM((4, 5, 2, NN), F32),
            pltpu.VMEM((CHIPS, SLOTS), jnp.int32),
            pltpu.SMEM((NN,), jnp.int32),
            pltpu.VMEM((4, CHIPS, NN), F32),
            pltpu.VMEM((8, 4, NN), F32),
            pltpu.SemaphoreType.DMA((5,)),
            pltpu.VMEM((SLOTS, 8, NN), F32),
            pltpu.VMEM((SLOTS, 8, NN), F32),
            pltpu.VMEM((SLOTS, 8, NN), F32),
            pltpu.VMEM((8 * CHIPS, 2 * NN), BF16),
            pltpu.VMEM((8 * CHIPS, 2 * NN), BF16),
            pltpu.VMEM((256, 2 * NN), BF16),
            pltpu.VMEM((2 * SLOTS * CHIPS, LANES), BF16),
            pltpu.VMEM((2 * SLOTS * CHIPS, LANES), BF16),
            pltpu.VMEM((256, LANES), BF16),
            message, message, message, message, message, message,
            pltpu.VMEM((3, 32, 512), F32),
            pltpu.VMEM((3, 32, 512), F32),
            pltpu.VMEM((12, 32, 128), F32),
            pltpu.SemaphoreType.DMA((2,)),
            pltpu.SemaphoreType.DMA((2,)),
            pltpu.SemaphoreType.DMA((3,)),
            pltpu.SemaphoreType.DMA((3,)),
            pltpu.SemaphoreType.DMA((3,)),
            pltpu.SemaphoreType.DMA((3,)),
        ],
        compiler_params=pltpu.CompilerParams(collective_id=0, has_side_effects=True, vmem_limit_bytes=62 << 20),
    )(spectrum, wave_slot.reshape(CHIPS, SLOTS), wave_slot, jnp.asarray(coarse), jnp.asarray(fine))


def solution(mesh):
    return jax.shard_map(
        on_device,
        mesh=mesh,
        in_specs=(P("lev", "grp", None, None), P()),
        out_specs=(P("lev", "grp", None, None), P("lev", "grp", None)),
        check_vma=False,
    )
```

```python
import functools
import math

import jax
import jax.numpy as jnp
import numpy as np
from jax import lax
from jax.experimental import pallas as pl
from jax.experimental.pallas import tpu as pltpu
from jax.sharding import PartitionSpec as P

NLON = 1440
LANES = 1536
NN = 640
NLAT = 1024
CHIPS = 64
SLOTS = 10
MESH = pl.DeviceIdType.MESH
F32 = jnp.float32
BF16 = jnp.bfloat16


def meridional_parts():
    chips = np.arange(CHIPS)
    coarse, fine = [], []
    odd_rows = 16 * np.arange(2)[:, None] + 2 * np.arange(8)[None, :] + 1
    for shift in range(2):
        k = np.arange(NN) + shift
        a = 2.0 * np.pi * ((chips[:, None] * k[None, :]) % 128) / 128.0
        b = np.pi * ((odd_rows[:, :, None] * k) % 4096) / 2048.0
        coarse += [np.cos(a), np.sin(a)]
        fine += [np.cos(b), np.sin(b)]
    return np.stack(coarse).astype(np.float32), np.stack(fine, axis=2).astype(np.float32)


def split(value):
    high = value.astype(BF16)
    return high, (value - high.astype(F32)).astype(BF16)


def dot_nn(a, b):
    return lax.dot_general(a, b, (((1,), (0,)), ((), ())), preferred_element_type=F32)


def dot_nt(a, b):
    return lax.dot_general(a, b, (((1,), (1,)), ((), ())), preferred_element_type=F32)


def cos_sin(steps):
    turn = steps - 1440.0 * jnp.floor((steps + 0.5) * (1.0 / 1440.0))
    quarter = jnp.floor((turn + 180.0) * (1.0 / 360.0) + 1e-4)
    t = (turn - 360.0 * quarter) * (2.0 * math.pi / 1440.0)
    u = t * t
    s = t * (1.0 + u * (-1.0 / 6 + u * (1.0 / 120 + u * (-1.0 / 5040 + u * (1.0 / 362880)))))
    c = 1.0 + u * (-0.5 + u * (1.0 / 24 + u * (-1.0 / 720 + u * (1.0 / 40320 + u * (-1.0 / 3628800)))))
    swap = (quarter == 1.0) | (quarter == 3.0)
    cos, sin = jnp.where(swap, s, c), jnp.where(swap, c, s)
    cos = jnp.where((quarter == 1.0) | (quarter == 2.0), -cos, cos)
    sin = jnp.where((quarter == 2.0) | (quarter == 3.0), -sin, sin)
    return cos, sin


def kernel(
    x_in, waves_in, scalars_in, coarse_in, fine_in,
    new_ref, products_ref,
    x_ref, waves_ref, wave_scalars, coarse_ref, fine_ref, load_sem,
    spec, part, part_in, mer_hi, mer_lo, weights_x, lon_hi, lon_lo, weights_p,
    send1, recv1, send2, recv2, send3, recv3, grid, grid_in, final,
    pair_send, pair_recv, all_send, all_recv, lev_send, lev_recv,
):
    me, level = lax.axis_index("grp"), lax.axis_index("lev")
    core, chip = lax.rem(me, 2), me // 2
    sibling = {"grp": 2 * chip + 1 - core}
    partner = {"lev": lax.rem(level + 2, 4)}

    chip_z = lax.rem(chip, 16)
    chip_rows = [16 * lax.rem(chip // 16 + along_x, 4) for along_x in range(4)]

    def each_peer(act):
        def plane(along_z, first_x):
            z = lax.rem(chip_z + along_z, 16)
            for along_x in range(3, first_x - 1, -1):
                act(chip_rows[along_x] + z)

        plane(8, 0)

        @pl.loop(1, 8)
        def _(turn):
            plane(8 - turn, 0)
            plane(8 + turn, 0)

        plane(0, 1)

    loads = [
        pltpu.make_async_copy(source, target, load_sem.at[index])
        for index, (source, target) in enumerate((
            (x_in, x_ref), (scalars_in, wave_scalars), (coarse_in, coarse_ref), (fine_in.at[core], fine_ref),
            (waves_in, waves_ref)))]
    for load in loads:
        load.start()
    barrier = pltpu.get_barrier_semaphore()

    each_peer(lambda to: pl.semaphore_signal(barrier, inc=1, device_id={"grp": 2 * to + core}, device_id_type=MESH))
    pl.semaphore_signal(barrier, inc=1, device_id=sibling, device_id_type=MESH)
    pl.semaphore_signal(barrier, inc=1, device_id=partner, device_id_type=MESH)

    loads[0].wait()
    loads[1].wait()
    for s in range(5):
        for c in range(2):
            spec[5 * core + s, 4 * c:4 * c + 4, :] = x_ref[:, s, c, :]

    loads[2].wait()
    loads[3].wait()
    @pl.loop(0, 8)
    def _(row):
        fine = fine_ref[row]
        for parity in range(2):
            fc, fs = fine[2 * parity:2 * parity + 1], fine[2 * parity + 1:2 * parity + 2]
            for block in range(4):
                rows = slice(16 * block, 16 * block + 16)
                cc, cs = coarse_ref[2 * parity, rows, :], coarse_ref[2 * parity + 1, rows, :]
                value = cc * fc - cs * fs if parity == 0 else cs * fc + cc * fs
                high, low = split(value)
                where = pl.ds(pl.multiple_of(row * CHIPS + 16 * block, 16), 16)
                columns = slice(NN * parity, NN * parity + NN)
                mer_hi[where, columns] = high
                mer_lo[where, columns] = low

    loads[4].wait()
    lane = lax.broadcasted_iota(jnp.int32, (16, 128), 1)
    lane_f = lane.astype(F32)
    for s in range(SLOTS):
        @pl.loop(0, 4)
        def _(block):
            wave = waves_ref[pl.ds(pl.multiple_of(16 * block, 16), 16), s:s + 1].astype(F32) + jnp.zeros((16, 128), F32)
            cos, sin = cos_sin(wave * lane_f)
            turn_cos, turn_sin = cos_sin(wave * 128.0)
            first = pl.multiple_of(s * CHIPS + 16 * block, 16)
            second = pl.multiple_of((SLOTS + s) * CHIPS + 16 * block, 16)
            for a in range(LANES // 128):
                columns = slice(128 * a, 128 * a + 128)
                put_cos, put_sin = cos, -sin
                if 128 * a + 128 > NLON:
                    inside = lane < NLON - 128 * a
                    put_cos, put_sin = jnp.where(inside, put_cos, 0.0), jnp.where(inside, put_sin, 0.0)
                lon_hi[pl.ds(first, 16), columns], lon_lo[pl.ds(first, 16), columns] = split(put_cos)
                lon_hi[pl.ds(second, 16), columns], lon_lo[pl.ds(second, 16), columns] = split(put_sin)
                if 128 * a + 128 < LANES:
                    cos, sin = cos * turn_cos - sin * turn_sin, sin * turn_cos + cos * turn_sin

    weights_x[...] = jnp.zeros_like(weights_x)
    weights_p[...] = jnp.zeros_like(weights_p)

    pl.semaphore_wait(barrier, CHIPS + 1)

    def pair_copy(index, source, target):
        return pltpu.make_async_remote_copy(
            src_ref=source, dst_ref=target, send_sem=pair_send.at[index], recv_sem=pair_recv.at[index],
            device_id=sibling, device_id_type=MESH)

    mine = spec.at[pl.ds(5 * core, 5)]
    copy = pair_copy(0, mine, mine)
    copy.start()
    copy.wait()

    degree = lax.broadcasted_iota(jnp.int32, (8, NN), 1)
    lane64 = lax.broadcasted_iota(jnp.int32, (CHIPS, 128), 1)
    lane8 = lax.broadcasted_iota(jnp.int32, (8, 128), 1)
    sub8 = lax.broadcasted_iota(jnp.int32, (8, 128), 0)

    def slot_wave(s):
        return wave_scalars[SLOTS * chip + s]

    def start(index, half, out, inbox):
        slot = 2 * index + half

        def send(to):
            pltpu.make_async_remote_copy(
                src_ref=out.at[half, to], dst_ref=inbox.at[half, chip],
                send_sem=all_send.at[slot], recv_sem=all_recv.at[slot],
                device_id={"grp": 2 * to + core}, device_id_type=MESH).start()

        each_peer(send)

        inbox[half, chip] = out[half, chip]

    def arrive(index, half, out, inbox):
        slot = 2 * index + half
        arrived = inbox.at[half, pl.ds(0, CHIPS - 1)]
        pltpu.make_async_copy(arrived, arrived, all_recv.at[slot]).wait()
        left = out.at[half, pl.ds(0, CHIPS - 1)]
        pltpu.make_async_copy(left, left, all_send.at[slot]).wait()

    def meridional_synth(index, source, out, inbox):
        for parity in range(2):
            for two in range(5):
                rows = []
                for s in (2 * two, 2 * two + 1):
                    wave = slot_wave(s)
                    odd = wave % 2
                    chosen = odd if parity else 1 - odd
                    scale = chosen.astype(F32) * jnp.where(wave == 0, 1.0 / NN, 2.0 / NN)
                    rows.append(jnp.where(degree >= wave, source[s] * scale, 0.0))
                high, low = split(jnp.concatenate(rows, axis=0))
                columns = slice(NN * parity, NN * parity + NN)
                weights_x[16 * two:16 * two + 16, columns] = high
                weights_x[128 + 16 * two:128 + 16 * two + 16, columns] = low
        for half in range(2):
            part_rows = slice(256 * half, 256 * half + 256)
            both = dot_nt(mer_hi[part_rows, :], weights_x[...])
            value = both[:, :128] + both[:, 128:] + dot_nt(mer_lo[part_rows, :], weights_x[:128, :])
            tiles = [None] * 3

            def put(t, piece):
                tiles[t] = piece if tiles[t] is None else tiles[t] + piece

            for row in range(4):
                t, offset = divmod(80 * row, 128)
                piece = value[CHIPS * row:CHIPS * row + CHIPS, :]
                if offset:
                    piece = pltpu.roll(piece, offset, 1)
                if offset + 80 > 128:
                    put(t, jnp.where(lane64 >= offset, piece, 0.0))
                    put(t + 1, jnp.where(lane64 < offset, piece, 0.0))
                else:
                    put(t, piece)
            for t in range(3):
                out[half, :, t, :] = tiles[t]
            start(index, half, out, inbox)

    def turned(inbox, half):
        result = []
        for t in range(3):
            block = inbox[half, :, t, :]
            result.append(jnp.concatenate([block, block], axis=0).T)
        return result

    def longitude_operand(inbox, half):
        tiles = turned(inbox, half)

        def group(row, s):
            t, offset = divmod(80 * row + 8 * s, 128)
            return tiles[t][offset:offset + 8, :]

        real, imag = [], []
        for pair in range(2):
            real_row, imag_row = [], []
            for two in range(5):
                a, b = (
                    jnp.where(lane8 < 64, group(row, 2 * two), group(row, 2 * two + 1))
                    for row in (2 * pair, 2 * pair + 1))
                real_row.append(jnp.where(sub8 < 4, a, pltpu.roll(b, 4, 0)))
                imag_row.append(jnp.where(sub8 < 4, pltpu.roll(a, 4, 0), b))
            real.append(jnp.concatenate(real_row, axis=1))
            imag.append(jnp.concatenate(imag_row, axis=1))
        value = jnp.concatenate([jnp.concatenate(real, axis=0), jnp.concatenate(imag, axis=0)], axis=1)
        return split(value)

    def longitude_synth(high, low, columns):
        both = dot_nn(jnp.concatenate([high, low], axis=0), lon_hi[:, columns])
        return both[:16] + both[16:] + dot_nn(high, lon_lo[:, columns])

    meridional_synth(0, spec, send1, recv1)
    copies = []
    for half in range(2):
        arrive(0, half, send1, recv1)
        high, low = longitude_operand(recv1, half)
        for a in range(3):
            slot = 3 * half + a
            grid[slot] = longitude_synth(high, low, slice(512 * a, 512 * a + 512))
            copy = pltpu.make_async_remote_copy(
                src_ref=grid.at[slot], dst_ref=grid_in.at[slot], send_sem=lev_send.at[slot], recv_sem=lev_recv.at[slot],
                device_id=partner, device_id_type=MESH)
            copy.start()
            copies.append(copy)

    for half in range(2):
        for a in range(3):
            slot = 3 * half + a
            copies[slot].wait()
            here = grid[slot]
            high, low = split(here * grid_in[slot] + here)
            weights_p[0:16, 512 * a:512 * a + 512] = high
            weights_p[128:144, 512 * a:512 * a + 512] = low
        both = dot_nt(lon_hi[...], weights_p[...])
        value = both[:, :128] + both[:, 128:] + dot_nt(lon_lo[...], weights_p[:128, :])
        for t in range(3):
            tile = None
            for s in range(4 * t, min(4 * t + 4, SLOTS)):
                for c in range(2):
                    first = (c * SLOTS + s) * CHIPS
                    piece = value[first:first + CHIPS, :]
                    offset = 32 * (s % 4) + 16 * c
                    piece = pltpu.roll(piece, offset, 1) if offset else piece
                    tile = piece if tile is None else tile + piece
            send2[half, :, t, :] = tile
        start(1, half, send2, recv2)

    value = None
    for half in range(2):
        arrive(1, half, send2, recv2)
        tiles = turned(recv2, half)
        rows = []
        for s in range(SLOTS):
            row = []
            for pair in range(2):
                first = 32 * (s % 4) + 8 * pair
                a, b = tiles[s // 4][first:first + 8, :], tiles[s // 4][first + 16:first + 24, :]
                left = jnp.where(sub8 < 4, a, pltpu.roll(b, 4, 0))
                right = jnp.where(sub8 < 4, pltpu.roll(a, 4, 0), b)
                row.append(jnp.where(lane8 < 64, left, right))
            rows.append(jnp.concatenate(row, axis=1))
        high, low = split(jnp.concatenate(rows, axis=0))
        part_rows = slice(256 * half, 256 * half + 256)
        both = dot_nn(jnp.concatenate([high, low], axis=0), mer_hi[part_rows, :])
        term = both[:80] + both[80:] + dot_nn(high, mer_lo[part_rows, :])
        value = term if value is None else value + term
    for s in range(SLOTS):
        wave = slot_wave(s)
        odd = (wave % 2).astype(F32)
        chosen = value[8 * s:8 * s + 8, :NN] * (1.0 - odd) + value[8 * s:8 * s + 8, NN:] * odd
        part[s] = jnp.where(degree >= wave, chosen * (2.0 * NN / NLAT / NLON), 0.0)
    copy = pair_copy(1, part, part_in)
    copy.start()
    copy.wait()
    for s in range(SLOTS):
        spec[s] = part[s] + part_in[s]
    for s in range(5):
        for c in range(2):
            new_ref[:, s, c, :] = spec[5 * core + s, 4 * c:4 * c + 4, :]

    meridional_synth(2, spec, send3, recv3)
    for half in range(2):
        arrive(2, half, send3, recv3)
        high, low = longitude_operand(recv3, half)
        for a in range(3):
            value = longitude_synth(high, low, slice(512 * a, 512 * a + 512))
            for b in range(4):
                tile = 4 * a + b
                width = min(128, NLON - 128 * tile)
                final[tile, 16 * half:16 * half + 16, :] = value[:, 128 * b:128 * b + 128]
                if half:
                    for l in range(4):
                        products_ref[l, :, 128 * tile:128 * tile + width] = final[tile, pl.ds(l, 8, stride=4), :][:, :width]


def on_device(spectrum, wave_slot):
    coarse, fine = meridional_parts()
    vmem, anywhere = pl.BlockSpec(memory_space=pltpu.VMEM), pl.BlockSpec(memory_space=pl.ANY)
    message = pltpu.VMEM((2, CHIPS, 3, 128), F32)
    return pl.pallas_call(
        kernel,
        out_shape=(
            jax.ShapeDtypeStruct((4, 5, 2, NN), F32),
            jax.ShapeDtypeStruct((4, 8, NLON), F32),
        ),
        in_specs=[anywhere] * 5,
        out_specs=(vmem, vmem),
        scratch_shapes=[
            pltpu.VMEM((4, 5, 2, NN), F32),
            pltpu.VMEM((CHIPS, SLOTS), jnp.int32),
            pltpu.SMEM((NN,), jnp.int32),
            pltpu.VMEM((4, CHIPS, NN), F32),
            pltpu.VMEM((8, 4, NN), F32),
            pltpu.SemaphoreType.DMA((5,)),
            pltpu.VMEM((SLOTS, 8, NN), F32),
            pltpu.VMEM((SLOTS, 8, NN), F32),
            pltpu.VMEM((SLOTS, 8, NN), F32),
            pltpu.VMEM((8 * CHIPS, 2 * NN), BF16),
            pltpu.VMEM((8 * CHIPS, 2 * NN), BF16),
            pltpu.VMEM((256, 2 * NN), BF16),
            pltpu.VMEM((2 * SLOTS * CHIPS, LANES), BF16),
            pltpu.VMEM((2 * SLOTS * CHIPS, LANES), BF16),
            pltpu.VMEM((256, LANES), BF16),
            message, message, message, message, message, message,
            pltpu.VMEM((6, 16, 512), F32),
            pltpu.VMEM((6, 16, 512), F32),
            pltpu.VMEM((12, 32, 128), F32),
            pltpu.SemaphoreType.DMA((2,)),
            pltpu.SemaphoreType.DMA((2,)),
            pltpu.SemaphoreType.DMA((6,)),
            pltpu.SemaphoreType.DMA((6,)),
            pltpu.SemaphoreType.DMA((6,)),
            pltpu.SemaphoreType.DMA((6,)),
        ],
        compiler_params=pltpu.CompilerParams(collective_id=0, has_side_effects=True, vmem_limit_bytes=62 << 20),
    )(spectrum, wave_slot.reshape(CHIPS, SLOTS), wave_slot, jnp.asarray(coarse), jnp.asarray(fine))


def solution(mesh):
    return jax.shard_map(
        on_device,
        mesh=mesh,
        in_specs=(P("lev", "grp", None, None), P()),
        out_specs=(P("lev", "grp", None, None), P("lev", "grp", None)),
        check_vma=False,
    )
```
